256 devices in a mesh: row: 8 (over y, core), col: 32 (over x, z).
Axes of the slice: x: 4, y: 4, z: 8, core: 2. Of those that a mesh axis runs over, the one named last changes fastest.
Arguments:
- features: bfloat16 [65536, 512], P(('row', 'col')), may hold values from -6 to 6
- memory: float32 [65536, 512], P(('col', 'row')), may hold values from -1 to 1
- tile_values: bfloat16 [8, 32, 128, 128, 128], P('row', 'col'), as said below
- tile_rows: int32 [8, 32, 128], P('row', 'col'), may hold values from 0 to 15, as said below
- tile_cols: int32 [8, 32, 128], P('row', 'col'), may hold values from 0 to 63
- tile_count: int32 [8, 32], P('row', 'col'), may hold values from 16 to 128, as said below
- conv_weight: bfloat16 [512, 512], replicated, may hold values from -0.25 to 0.25
- conv_bias: float32 [512], replicated, may hold values from -3 to 3
- input_weight: bfloat16 [512, 1536], replicated, may hold values from -0.25 to 0.25
- input_bias: float32 [1536], replicated, may hold values from -3 to 3
- hidden_weight: bfloat16 [512, 1536], replicated, may hold values from -0.25 to 0.25
- hidden_bias: float32 [1536], replicated, may hold values from -3 to 3
Outputs:
- new_memory: float32 [65536, 512], P(('col', 'row'))
The draws below stay inside these ranges and needn't reach their ends.
Inputs may be any that keep to these rules, and one draw needn't show every extreme that they name: `tile_values`: edge weights are nonnegative. For each device pair (r, c) the 128 pairs (tile_rows, tile_cols) are distinct. `tile_count`: in every draw some device pair has all 128 slots live.
All inputs are finite; a program needn't handle non-finite values.
Results may differ from the reference program's by a relative error of at most 0.017.
Values may be sent and summed in bfloat16 or wider, within the bound.
A program may use at most 128 MiB of HBM per device.

```python
import math
import jax
import jax.numpy as jnp
from jax import lax

F = 512
TILE = 128
NODES = 65536
DST_GROUP = 2048
SRC_GROUP = 8192
ROW_BLOCKS = 16
COL_BLOCKS = 64
SLOTS = 128
N_ROW = 8
N_COL = 32


def tile_layout(key):
    layout_key = jax.random.fold_in(key, 7)
    device_keys = jax.random.split(layout_key, N_ROW * N_COL)

    def one_device(device_key):
        return jax.random.permutation(device_key, ROW_BLOCKS * COL_BLOCKS)[:SLOTS]
    chosen = jax.vmap(one_device)(device_keys).astype(jnp.int32).reshape(N_ROW, N_COL, SLOTS)
    return (chosen // COL_BLOCKS, chosen % COL_BLOCKS)


def draw_tile_rows(key, part):
    return tile_layout(key)[0]


def draw_tile_cols(key, part):
    return tile_layout(key)[1]


def draw_tile_count(key, part):
    device_total = N_ROW * N_COL
    shifts = jax.random.randint(jax.random.fold_in(key, 21), (device_total,), 0, 3)
    ceiling = jnp.right_shift(jnp.full((device_total,), SLOTS, jnp.int32), shifts.astype(jnp.int32))
    shortfall = jax.random.randint(jax.random.fold_in(key, 22), (device_total,), 0, ceiling // 2 + 1)
    counts = ceiling - shortfall
    busiest = jax.random.randint(jax.random.fold_in(key, 23), (), 0, device_total)
    lightest = (busiest + 1 + jax.random.randint(jax.random.fold_in(key, 24), (), 0, device_total - 1)) % device_total
    positions = jnp.arange(device_total)
    counts = jnp.where(positions == busiest, SLOTS, counts)
    counts = jnp.where(positions == lightest, SLOTS // 8, counts)
    return counts.reshape(N_ROW, N_COL).astype(jnp.int32)


def draw_tile_values(key, part):
    row_ids, col_ids = tile_layout(key)
    offsets = jnp.arange(TILE)
    group_col = jnp.arange(N_COL)[None, :, None, None]
    group_row = jnp.arange(N_ROW)[:, None, None, None]
    dst_index = group_col * DST_GROUP + row_ids[..., None] * TILE + offsets
    src_index = group_row * SRC_GROUP + col_ids[..., None] * TILE + offsets
    lowest, highest = (0.2, 5.0)
    dst_scale = jnp.exp(jax.random.uniform(jax.random.fold_in(key, 31), (NODES,), jnp.float32, math.log(lowest), math.log(highest)))
    src_scale = jnp.exp(jax.random.uniform(jax.random.fold_in(key, 32), (NODES,), jnp.float32, math.log(lowest), math.log(highest)))
    growth = 1.0 + 2.0 * jnp.arange(N_COL, dtype=jnp.float32) / (N_COL - 1)
    dst_part = dst_scale[dst_index] * growth[None, :, None, None]
    src_part = src_scale[src_index]
    full_shape = (N_ROW, N_COL, SLOTS, TILE, TILE)
    present = jax.random.bernoulli(jax.random.fold_in(key, 33), 0.3, full_shape)
    jitter = jax.random.uniform(jax.random.fold_in(key, 34), full_shape, jnp.float32, 0.5, 1.5)
    values = jnp.where(present, dst_part[..., :, None] * src_part[..., None, :] * jitter, jnp.float32(0.0))
    return values.astype(jnp.bfloat16)


def shard_levels(stream_key, extent, cuts, smallest, high):
    gain, own = 1.0, jax.random.fold_in(stream_key, 6)
    for dim, shards_of in cuts:
        draws = jnp.exp(jax.random.uniform(jax.random.fold_in(own, dim), (shards_of,), jnp.float32, smallest / len(cuts), high / len(cuts)))
        gain = gain * jnp.repeat(draws, extent[dim] // shards_of).reshape([-1 if axis == dim else 1 for axis in range(len(extent))])
    return gain


def centred(own_key, dims, scale, bound, cuts=(), kind=jnp.bfloat16):
    gain = shard_levels(own_key, dims, cuts, -0.22, 0.18) if cuts else 1.0
    array = jax.random.normal(own_key, dims, jnp.float32) * scale * gain
    return jnp.minimum(jnp.maximum(array, -bound), bound).astype(kind)


def setup_inputs(seed: int = 0) -> dict:
    streams_of = jax.random.split(jax.random.key(seed), 13)
    features = centred(streams_of[0], (NODES, F), 1.0, 6.0, ((0, 256),))
    memory = jnp.clip(jax.random.uniform(streams_of[1], (NODES, F), jnp.float32, -1.0, 1.0) * shard_levels(streams_of[1], (NODES, F), ((0, 256),), -0.4, 0.0), -1.0, 1.0)
    tile_values = draw_tile_values(jax.random.fold_in(streams_of[12], 71), 0)
    tile_rows = draw_tile_rows(jax.random.fold_in(streams_of[12], 71), 0)
    tile_cols = draw_tile_cols(jax.random.fold_in(streams_of[12], 71), 0)
    tile_count = draw_tile_count(jax.random.fold_in(streams_of[12], 71), 0)
    conv_weight = centred(streams_of[6], (F, F), F ** -0.5, 0.25)
    conv_bias = centred(streams_of[7], (F,), 0.5, 3.0, (), jnp.float32)
    input_weight = centred(streams_of[8], (F, 3 * F), F ** -0.5, 0.25)
    input_bias = centred(streams_of[9], (3 * F,), 0.5, 3.0, (), jnp.float32)
    hidden_weight = centred(streams_of[10], (F, 3 * F), F ** -0.5, 0.25)
    hidden_bias = centred(streams_of[11], (3 * F,), 0.5, 3.0, (), jnp.float32)
    return {"features": features, "memory": memory, "tile_values": tile_values, "tile_rows": tile_rows, "tile_cols": tile_cols, "tile_count": tile_count, "conv_weight": conv_weight, "conv_bias": conv_bias, "input_weight": input_weight, "input_bias": input_bias, "hidden_weight": hidden_weight, "hidden_bias": hidden_bias}


norm_epsilon = 1e-06

def gru_update(message, memory, input_weight, input_bias, hidden_weight, hidden_bias):
    width = memory.shape[1]
    from_input = jnp.dot(message, input_weight, preferred_element_type=jnp.float32) + input_bias
    held = memory.astype(jnp.bfloat16)
    from_memory = jnp.dot(held, hidden_weight, preferred_element_type=jnp.float32) + hidden_bias
    reset = jax.nn.sigmoid(from_input[:, :width] + from_memory[:, :width])
    update = jax.nn.sigmoid(from_input[:, width:2 * width] + from_memory[:, width:2 * width])
    candidate = jnp.tanh(from_input[:, 2 * width:] + reset * from_memory[:, 2 * width:])
    return (1.0 - update) * candidate + update * memory

def device_product(tile_data, row_ids, col_ids, live_count, panel):
    live = jnp.arange(tile_data.shape[0]) < live_count
    tiles_wide = jnp.where(live[:, None, None], tile_data.astype(jnp.float32), jnp.float32(0.0))
    picked = panel[col_ids].astype(jnp.float32)
    products = jnp.einsum('tpq,tqf->tpf', tiles_wide, picked)
    return jnp.zeros((ROW_BLOCKS, TILE, F), jnp.float32).at[row_ids].add(products)

def reference(features, memory, tile_values, tile_rows, tile_cols, tile_count, conv_weight, conv_bias, input_weight, input_bias, hidden_weight, hidden_bias):
    live = jnp.arange(SLOTS)[None, None, :] < tile_count[:, :, None]
    column_sums = lax.optimization_barrier(jnp.sum(tile_values, axis=3, dtype=jnp.float32)) * live[..., None]
    group_index = jnp.broadcast_to(jnp.arange(N_ROW)[:, None, None], tile_cols.shape)
    out_degree = 1.0 + jnp.zeros((N_ROW, COL_BLOCKS, TILE), jnp.float32).at[group_index, tile_cols].add(column_sums)
    scaled = (features.reshape(N_ROW, COL_BLOCKS, TILE, F).astype(jnp.float32) * lax.rsqrt(out_degree)[..., None]).astype(jnp.bfloat16)

    def one_group(target):

        def one_source(source):
            return device_product(tile_values[source, target], tile_rows[source, target], tile_cols[source, target], tile_count[source, target], scaled[source])
        pieces = lax.map(one_source, jnp.arange(N_ROW))
        return lax.optimization_barrier(jnp.sum(pieces, axis=0))
    partial_value = lax.map(one_group, jnp.arange(N_COL)).reshape(NODES, F)
    normed = (partial_value / jnp.sqrt(lax.optimization_barrier(jnp.mean(partial_value * partial_value, axis=1, keepdims=True)) + norm_epsilon)).astype(jnp.bfloat16)
    message = jax.nn.relu(jnp.dot(normed, conv_weight, preferred_element_type=jnp.float32) + conv_bias).astype(jnp.bfloat16)
    return gru_update(message, memory, input_weight, input_bias, hidden_weight, hidden_bias)
```

```python
import functools

import jax
import jax.numpy as jnp
from jax import lax
from jax.experimental import pallas as pl
from jax.experimental.pallas import tpu as pltpu
from jax.sharding import PartitionSpec as P

norm_epsilon = 1e-06
NX, NZ = 4, 8
NY = 4
ROWS_A = 96
N_CHUNK = 2
GROUP = 2
MESH = pl.DeviceIdType.MESH
F32 = jnp.float32
BF16 = jnp.bfloat16


def block_units(f, part, rows):
    lo, hi = rows
    mid = (lo + hi) // 2
    units, at = {}, {(0, 0): []}
    n1, n2 = (NX, NZ) if part == 0 else (NZ, NX)
    first, second = ("x", "z") if part == 0 else ("z", "x")

    def offset(d1, d2):
        return (d1, d2) if part == 0 else (d2, d1)

    def ring(axis, n, place):
        for d in range(1, n // 2):
            for sign in (1, -1):
                key = (f, part, *place(sign * d), 2)
                units[key] = (axis, sign, lo, hi, list(at[place(sign * (d - 1))]))
                at[place(sign * d)] = [key]
        far = place(n // 2)
        at[far] = []
        for half, (sign, a, b) in enumerate(((1, lo, mid), (-1, mid, hi))):
            key = (f, part, *far, half)
            units[key] = (axis, sign, a, b, list(at[place(sign * (n // 2 - 1))]))
            at[far].append(key)

    ring(first, n1, lambda d: offset(d, 0))
    for d1 in [0] + [s * d for d in range(1, n1 // 2) for s in (1, -1)] + [n1 // 2]:
        ring(second, n2, lambda d, d1=d1: offset(d1, d))
    return units, at


def make_plan(block_rows, width):
    units, arrivals = {}, {}
    for f in range(N_CHUNK):
        for part, rows in ((0, (0, ROWS_A)), (1, (ROWS_A, block_rows))):
            more, at = block_units(f, part, rows)
            units.update(more)
            for place, keys in at.items():
                arrivals.setdefault((f, *place), []).extend(keys)
    per_row = width // N_CHUNK * 2 * 2 / 90e3
    hop = 0.9
    length = {k: (u[3] - u[2]) * per_row for k, u in units.items()}
    after = {k: [] for k in units}
    for k, u in units.items():
        for p in u[4]:
            after[p].append(k)
    tail = {}

    def tail_of(k):
        if k not in tail:
            tail[k] = length[k] + hop + max([tail_of(j) for j in after[k]], default=0.0)
        return tail[k]

    order = sorted(units, key=lambda k: (k[0], -tail_of(k), k))
    lanes = [(a, s) for a in "xz" for s in (1, -1)]
    arrived, free, busy = {}, dict.fromkeys(lanes, 0.0), {lane: [] for lane in lanes}
    left = list(order)
    cost = 16.5 / (N_CHUNK * 16) * GROUP / 2
    tasks = [
        ["sums", 0, None, 2.0, 1.0],
        ["sums", 1, "sums0", 0.0, 1.0],
        ["degrees", 0, "sums1", 0.0, 1.5],
        ["degrees", 1, "degrees0", 5.0, 1.5],
        ["scale", 0, "degrees1", 4.0, 1.0],
        ["scale", 1, "scale0", 0.0, 1.0],
    ]
    for f in range(N_CHUNK):
        tasks += [
            ["reduce", 4 * f, f"all{f}", 0.0, 0.5],
            ["reduce", 4 * f + 1, f"reduce{4 * f}", 3.5, 0.5],
            ["reduce", 4 * f + 2, f"reduce{4 * f + 1}", 5.0, 0.3],
            ["reduce", 4 * f + 3, f"reduce{4 * f + 2}", 5.0, 0.3],
        ]
    tasks.append(["held", 0, "scale1", 0.0, 2.0])
    sources = [p for p in arrivals if p not in [(f, 0, 0) for f in range(N_CHUNK)]]
    waiting = [(f, 0, 0) for f in range(N_CHUNK)] + sources
    count = dict.fromkeys(range(N_CHUNK), 0)
    done, steps, now = {}, [], 0.0
    while left or tasks or waiting:
        for lane in lanes:
            busy[lane] = [e for e in busy[lane] if e > now]
        pick = None
        for k in left:
            lane = units[k][:2]
            if len(busy[lane]) < 3 and all(arrived.get(p, 1e9) <= now for p in units[k][4]):
                pick = k
                break
        if pick is not None:
            lane = units[pick][:2]
            free[lane] = max(free[lane], now) + length[pick]
            busy[lane].append(free[lane])
            arrived[pick] = free[lane] + hop
            left.remove(pick)
            steps.append(("send", pick))
            now += 0.08
            continue
        task = next((t for t in tasks if t[2] is None and t[3] <= now or t[2] in done and done[t[2]] + t[3] <= now), None)
        if task is not None:
            tasks.remove(task)
            steps.append((task[0], task[1]))
            now += task[4]
            done[f"{task[0]}{task[1]}"] = now
            continue
        picked = None
        if "scale1" in done:
            for f in range(N_CHUNK):
                ready = [p for p in waiting if p[0] == f and all(arrived.get(k, 1e9) <= now for k in arrivals[p])]
                remaining = sum(p[0] == f for p in waiting)
                if len(ready) >= GROUP or ready and len(ready) == remaining:
                    ready.sort(key=lambda p: max([arrived[k] for k in arrivals[p]], default=0.0))
                    picked = ready[:GROUP]
                    break
        if picked:
            for p in picked:
                waiting.remove(p)
            f = picked[0][0]
            steps.append(("multiply", (f, tuple(p[1:] for p in picked), count[f] == 0)))
            count[f] += len(picked)
            now += cost
            if not any(p[0] == f for p in waiting):
                done[f"all{f}"] = now
            continue
        now += 0.05
    return units, arrivals, steps, now


def kernel(
    plan, inv, cols_s, count_s, cols_v, feats, memory_v, tiles_h, conv_w, in_w, hid_w, conv_b, in_b, hid_b, out,
    panel, tiles, acc, sums, deg_out, deg_in, scales, cw, iw, hw, held, own,
    s1, r1, s2, r2, s3, r3, message,
    send_sem, recv_sem, dsem_s, dsem_r, load_sem, rs_s, rs_r,
):
    units, arrivals, steps = plan
    index = {k: i for i, k in enumerate(units)}
    slots, tile = tiles_h.shape[0], tiles_h.shape[1]
    block_rows, width = feats.shape
    wide = width // N_CHUNK
    n_col, n_row = NX * NZ, 2 * NY
    col_blocks = n_col * block_rows // tile
    group_rows = n_row * block_rows
    r = lax.axis_index("row")
    c = lax.axis_index("col")
    x, z = lax.div(c, NZ), lax.rem(c, NZ)
    y, core = lax.div(r, 2), lax.rem(r, 2)

    def col_at(dx, dz):
        return lax.rem(x + (dx + NX), NX) * NZ + lax.rem(z + (dz + NZ), NZ)

    def row_at(dy, other):
        return lax.rem(y + (dy + NY), NY) * 2 + (1 - core if other else core)

    half_slots = slots // 2
    loads = [
        pltpu.make_async_copy(tiles_h.at[pl.ds(i * half_slots, half_slots)], tiles.at[pl.ds(i * half_slots, half_slots)], load_sem.at[i])
        for i in range(2)
    ]
    loads += [pltpu.make_async_copy(a, b, load_sem.at[2 + i]) for i, (a, b) in enumerate(((hid_w, hw), (conv_w, cw), (in_w, iw)))]
    for copy in loads:
        copy.start()

    barrier = pltpu.get_barrier_semaphore()

    @pl.loop(1, n_col)
    def _(i):
        pl.semaphore_signal(barrier, inc=1, device_id=(r, lax.rem(c + i, n_col)), device_id_type=MESH)

    for dy, other in ((0, True), (1, False), (-1, False)):
        pl.semaphore_signal(barrier, inc=1, device_id=(row_at(dy, other), c), device_id_type=MESH)
    for f in range(N_CHUNK):
        panel[f, c] = feats[:, f * wide : (f + 1) * wide]
    pl.semaphore_wait(barrier, n_col - 1 + 3)

    def arrival(key):
        f, _, dx, dz, _ = key
        _, _, lo, hi, _ = units[key]
        spot = panel.at[f, col_at(dx, dz), pl.ds(lo, hi - lo)]
        i = index[key]
        return pltpu.make_async_remote_copy(
            spot, spot, send_sem.at[i], recv_sem.at[i], device_id=(r, c), device_id_type=MESH
        )

    def sending(key):
        f, _, dx, dz, _ = key
        axis, sign, lo, hi, _ = units[key]
        sx, sz = (sign, 0) if axis == "x" else (0, sign)
        spot = panel.at[f, col_at(dx - sx, dz - sz), pl.ds(lo, hi - lo)]
        i = index[key]
        return pltpu.make_async_remote_copy(
            spot, spot, send_sem.at[i], recv_sem.at[i], device_id=(r, col_at(-sx, -sz)), device_id_type=MESH
        )

    waited = set()

    def wait_for(keys):
        for k in keys:
            if k not in waited:
                waited.add(k)
                arrival(k).wait_recv()

    def column_sums(part):
        loads[part].wait()

        @pl.loop(0, half_slots // 8)
        def _(g):
            t0 = pl.multiple_of(part * half_slots + g * 8, 8)
            rows = [jnp.sum(tiles[t0 + k].astype(F32), axis=0, keepdims=True) for k in range(8)]
            sums[pl.ds(t0, 8), :] = jnp.concatenate(rows, axis=0)

    def degree_send(i, first):
        peer = lax.rem(c + i, n_col)
        if first:
            src, dst = deg_out.at[pl.ds(2 * peer, 2)], deg_in.at[c]
        else:
            src = dst = scales.at[pl.ds(2 * c, 2)]
        k = 0 if first else 1
        return pltpu.make_async_remote_copy(
            src, dst, dsem_s.at[k, i], dsem_r.at[k, i], device_id=(r, peer), device_id_type=MESH
        )

    def degrees(part):
        if part == 0:
            block = lax.broadcasted_iota(jnp.int32, (col_blocks, slots), 0)
            slot = lax.broadcasted_iota(jnp.int32, (col_blocks, slots), 1)
            picker = jnp.where((cols_v[...] == block) & (slot < count_s[0]), 1.0, 0.0).astype(F32)
            terms = jnp.dot(picker, sums[...], precision=lax.Precision.HIGHEST, preferred_element_type=F32)
            for b in range(col_blocks):
                deg_out[b] = terms[b : b + 1, :]
            deg_in[c] = deg_out[pl.ds(2 * c, 2)]

            @pl.loop(1, n_col)
            def _(i):
                degree_send(i, True).start()
        else:

            @pl.loop(1, n_col)
            def _(i):
                degree_send(i, True).wait_recv()

            total = jnp.sum(deg_in[...], axis=0)
            scales[pl.ds(2 * c, 2)] = lax.rsqrt(1.0 + total)

            @pl.loop(1, n_col)
            def _(i):
                degree_send(i, False).start()

    def scale(part):
        if part == 0:

            @pl.loop(1, n_col)
            def _(i):
                degree_send(i, False).wait_recv()

            tiles[slots] = jnp.zeros((tile, tile), BF16)

        @pl.loop(0, half_slots // 4)
        def _(g):
            for k in range(4):
                t = part * half_slots + g * 4 + k
                tiles[t] = (tiles[t].astype(F32) * scales[cols_s[t]]).astype(BF16)

    def multiply(f, places, first):
        m_blocks = 4
        spots = [col_at(*place) for place in places]

        @pl.loop(0, group_rows // (tile * m_blocks))
        def _(m):
            total = None
            for s in spots:
                lhs = []
                for a in range(m_blocks):
                    base = (m * m_blocks + a) * col_blocks + 2 * s
                    lhs.append(jnp.concatenate([tiles[inv[base]], tiles[inv[base + 1]]], axis=1))
                term = jnp.dot(jnp.concatenate(lhs, axis=0), panel[f, s], preferred_element_type=F32)
                total = term if total is None else total + term
            rows = pl.ds(pl.multiple_of(m * (m_blocks * tile), m_blocks * tile), m_blocks * tile)
            if first:
                acc[f, rows] = total
            else:
                acc[f, rows] += total

    half = block_rows // 2

    def owner_rows(rr, part=None):
        start = pl.multiple_of(rr * block_rows, block_rows)
        if part is None:
            return pl.ds(start, block_rows)
        return pl.ds(start + part * half, half)

    def rs_core(f):
        return pltpu.make_async_remote_copy(
            s1.at[f], r1.at[f], rs_s.at[f, 0], rs_r.at[f, 0], device_id=(row_at(0, True), c), device_id_type=MESH
        )

    def rs_first(f, up):
        return pltpu.make_async_remote_copy(
            s2.at[f, up], r2.at[f, up], rs_s.at[f, 1 + up], rs_r.at[f, 1 + up],
            device_id=(row_at(1 - 2 * up, False), c), device_id_type=MESH,
        )

    def rs_second(f, up):
        return pltpu.make_async_remote_copy(
            s3.at[f, up], r3.at[f, up], rs_s.at[f, 3 + up], rs_r.at[f, 3 + up],
            device_id=(row_at(1 - 2 * up, False), c), device_id_type=MESH,
        )

    def reduce(f, stage):
        if stage == 0:
            for q in range(NY):
                s1[f, q] = acc[f, owner_rows(q * 2 + (1 - core))].astype(BF16)
            rs_core(f).start()
        elif stage == 1:
            rs_core(f).wait_recv()

            def pair(dy, part):
                rr = row_at(dy, False)
                q = lax.rem(y + (dy + NY), NY)
                return acc[f, owner_rows(rr, part)] + r1[f, q, part * half : (part + 1) * half].astype(F32)

            for up in (0, 1):
                s2[f, up, 0] = pair(2, up).astype(BF16)
                s2[f, up, 1] = pair(1 - 2 * up, 1 - up).astype(BF16)
                rs_first(f, up).start()
            for up in (0, 1):
                own[f, up] = pair(1 - 2 * up, up)
                own[f, 2 + up] = pair(0, up)
        elif stage == 2:
            for up in (0, 1):
                rs_first(f, up).wait_recv()
                s3[f, up] = (own[f, up] + r2[f, up, 0].astype(F32)).astype(BF16)
                rs_second(f, up).start()
        else:
            for up in (0, 1):
                rs_second(f, up).wait_recv()
            for part in (0, 1):
                own[f, 2 + part] += r3[f, part].astype(F32) + r2[f, 1 - part, 1].astype(F32)

    def held_product():
        loads[2].wait()
        bias = hid_b[...]
        low = memory_v[...].astype(BF16)
        for j in range(3 * width // 256):
            part = slice(j * 256, (j + 1) * 256)
            term = jnp.dot(low, hw[:, part], preferred_element_type=F32) + bias[:, part]
            held[:, part] = term

    run = {
        "sums": column_sums,
        "degrees": degrees,
        "scale": scale,
        "held": lambda _: held_product(),
        "reduce": lambda k: reduce(k // 4, k % 4),
    }
    for what, arg in steps:
        if what == "send":
            wait_for(units[arg][4])
            sending(arg).start()
        elif what == "multiply":
            f, places, first = arg
            for place in places:
                wait_for(arrivals[(f, *place)])
            multiply(f, places, first)
        else:
            run[what](arg)

    loads[3].wait()
    loads[4].wait()
    for part in (0, 1):
        rows = slice(part * half, (part + 1) * half)
        owned = [own[f, 2 + part] for f in range(N_CHUNK)]
        square = sum(jnp.sum(o * o, axis=1, keepdims=True) for o in owned) * (1.0 / width)
        root = jnp.sqrt(square + norm_epsilon)
        normed = jnp.concatenate([(o / root).astype(BF16) for o in owned], axis=1)
        value = jnp.dot(normed, cw[...], preferred_element_type=F32) + conv_b[...]
        message[rows] = jnp.maximum(value, 0.0).astype(BF16)
    bias = in_b[...]
    told = message[...]
    for j in range(width // 128):
        low, mid, high = (slice(k * width + j * 128, k * width + (j + 1) * 128) for k in range(3))
        gates = [jnp.dot(told, iw[:, p], preferred_element_type=F32) + bias[:, p] for p in (low, mid, high)]
        reset = jax.nn.sigmoid(gates[0] + held[:, low])
        update = jax.nn.sigmoid(gates[1] + held[:, mid])
        candidate = jnp.tanh(gates[2] + reset * held[:, high])
        out[:, low] = (1.0 - update) * candidate + update * memory_v[:, low]

    for k in units:
        sending(k).wait_send()

    @pl.loop(1, n_col)
    def _(i):
        degree_send(i, True).wait_send()
        degree_send(i, False).wait_send()

    for f in range(N_CHUNK):
        rs_core(f).wait_send()
        for up in (0, 1):
            rs_first(f, up).wait_send()
            rs_second(f, up).wait_send()


def on_device(
    features, memory, tile_values, tile_rows, tile_cols, tile_count,
    conv_weight, conv_bias, input_weight, input_bias, hidden_weight, hidden_bias,
):
    own_rows, width = features.shape
    tiles = tile_values[0, 0]
    slots, tile = tiles.shape[0], tiles.shape[1]
    rows, cols, count = tile_rows[0, 0], tile_cols[0, 0], tile_count[0, 0]
    n_col, n_row = lax.axis_size("col"), lax.axis_size("row")
    row_blocks, col_blocks = own_rows * n_row // tile, own_rows * n_col // tile
    key = jnp.where(jnp.arange(slots) < count, rows * col_blocks + cols, -1)
    spot = jnp.arange(row_blocks * col_blocks)
    hit = key[None, :] == spot[:, None]
    inv = slots + jnp.sum(jnp.where(hit, jnp.arange(slots)[None, :] - slots, 0), axis=1)
    units, arrivals, steps, _ = make_plan(own_rows, width)
    wide = width // N_CHUNK
    half = own_rows // 2
    n = len(units)
    smem = pl.BlockSpec(memory_space=pltpu.SMEM)
    vmem = pl.BlockSpec(memory_space=pltpu.VMEM)
    hbm = pl.BlockSpec(memory_space=pl.ANY)
    return pl.pallas_call(
        functools.partial(kernel, (units, arrivals, steps)),
        out_shape=jax.ShapeDtypeStruct((own_rows, width), F32),
        in_specs=[smem, smem, smem, vmem, vmem, vmem, hbm, hbm, hbm, hbm, vmem, vmem, vmem],
        out_specs=vmem,
        scratch_shapes=[
            pltpu.VMEM((N_CHUNK, n_col, own_rows, wide), BF16),
            pltpu.VMEM((slots + 1, tile, tile), BF16),
            pltpu.VMEM((N_CHUNK, n_row * own_rows, wide), F32),
            pltpu.VMEM((slots, tile), F32),
            pltpu.VMEM((col_blocks, 1, tile), F32),
            pltpu.VMEM((n_col, 2, 1, tile), F32),
            pltpu.VMEM((col_blocks, 1, tile), F32),
            pltpu.VMEM((width, width), BF16),
            pltpu.VMEM((width, 3 * width), BF16),
            pltpu.VMEM((width, 3 * width), BF16),
            pltpu.VMEM((own_rows, 3 * width), F32),
            pltpu.VMEM((N_CHUNK, 4, half, wide), F32),
            pltpu.VMEM((N_CHUNK, NY, own_rows, wide), BF16),
            pltpu.VMEM((N_CHUNK, NY, own_rows, wide), BF16),
            pltpu.VMEM((N_CHUNK, 2, 2, half, wide), BF16),
            pltpu.VMEM((N_CHUNK, 2, 2, half, wide), BF16),
            pltpu.VMEM((N_CHUNK, 2, half, wide), BF16),
            pltpu.VMEM((N_CHUNK, 2, half, wide), BF16),
            pltpu.VMEM((own_rows, width), BF16),
            pltpu.SemaphoreType.DMA((n,)),
            pltpu.SemaphoreType.DMA((n,)),
            pltpu.SemaphoreType.DMA((2, n_col)),
            pltpu.SemaphoreType.DMA((2, n_col)),
            pltpu.SemaphoreType.DMA((5,)),
            pltpu.SemaphoreType.DMA((N_CHUNK, 5)),
            pltpu.SemaphoreType.DMA((N_CHUNK, 5)),
        ],
        compiler_params=pltpu.CompilerParams(
            collective_id=0, has_side_effects=True, vmem_limit_bytes=48 << 20
        ),
    )(
        inv, cols, count.reshape(1), cols.reshape(1, slots), features, memory, tiles,
        conv_weight, input_weight, hidden_weight,
        conv_bias.reshape(1, -1), input_bias.reshape(1, -1), hidden_bias.reshape(1, -1),
    )


def solution(mesh):
    placed = (
        P(("row", "col"), None),
        P(("col", "row"), None),
        P("row", "col", None, None, None),
        P("row", "col", None),
        P("row", "col", None),
        P("row", "col"),
        P(),
        P(),
        P(),
        P(),
        P(),
        P(),
    )
    return jax.shard_map(
        on_device, mesh=mesh, in_specs=placed, out_specs=P(("col", "row"), None), check_vma=False
    )
```

```python
import functools

import jax
import jax.numpy as jnp
from jax import lax
from jax.experimental import pallas as pl
from jax.experimental.pallas import tpu as pltpu
from jax.sharding import PartitionSpec as P

norm_epsilon = 1e-06
NX, NZ = 4, 8
NY = 4
ROWS_A = (96, 96)
N_CHUNK = 2
GROUP = 4
MESH = pl.DeviceIdType.MESH
F32 = jnp.float32
BF16 = jnp.bfloat16


def block_units(f, part, rows):
    lo, hi = rows
    mid = (lo + hi) // 2
    units, at = {}, {(0, 0): []}
    n1, n2 = (NX, NZ) if part == 0 else (NZ, NX)
    first, second = ("x", "z") if part == 0 else ("z", "x")

    def offset(d1, d2):
        return (d1, d2) if part == 0 else (d2, d1)

    def ring(axis, n, place):
        for d in range(1, n // 2):
            for sign in (1, -1):
                key = (f, part, *place(sign * d), 2)
                units[key] = (axis, sign, lo, hi, list(at[place(sign * (d - 1))]))
                at[place(sign * d)] = [key]
        far = place(n // 2)
        at[far] = []
        for half, (sign, a, b) in enumerate(((1, lo, mid), (-1, mid, hi))):
            key = (f, part, *far, half)
            units[key] = (axis, sign, a, b, list(at[place(sign * (n // 2 - 1))]))
            at[far].append(key)

    ring(first, n1, lambda d: offset(d, 0))
    for d1 in [0] + [s * d for d in range(1, n1 // 2) for s in (1, -1)] + [n1 // 2]:
        ring(second, n2, lambda d, d1=d1: offset(d1, d))
    return units, at


def make_plan(block_rows, width):
    units, arrivals = {}, {}
    for f in range(N_CHUNK):
        for part, rows in ((0, (0, ROWS_A[f])), (1, (ROWS_A[f], block_rows))):
            more, at = block_units(f, part, rows)
            units.update(more)
            for place, keys in at.items():
                arrivals.setdefault((f, *place), []).extend(keys)
    per_row = width // N_CHUNK * 2 * 2 / 90e3
    hop = 1.5
    length = {k: (u[3] - u[2]) * per_row for k, u in units.items()}
    after = {k: [] for k in units}
    for k, u in units.items():
        for p in u[4]:
            after[p].append(k)
    tail = {}

    def tail_of(k):
        if k not in tail:
            tail[k] = length[k] + hop + max([tail_of(j) for j in after[k]], default=0.0)
        return tail[k]

    order = sorted(units, key=lambda k: (k[0], -tail_of(k), k))
    lanes = [(a, s) for a in "xz" for s in (1, -1)]
    arrived, free, busy = {}, dict.fromkeys(lanes, 0.0), {lane: [] for lane in lanes}
    left = list(order)
    cost = 22.0 / (N_CHUNK * 32) * GROUP
    tasks = [
        ["sums", 0, None, 2.0, 1.0],
        ["sums", 1, "sums0", 0.0, 1.0],
        ["degrees", 0, "sums1", 0.0, 1.5],
        ["degrees", 1, "degrees0", 5.0, 1.5],
        ["scale", 0, "degrees1", 4.0, 1.0],
        ["scale", 1, "scale0", 0.0, 1.0],
    ]
    for f in range(N_CHUNK):
        tasks += [
            ["reduce", 6 * f, f"all{f}", 0.0, 0.5],
            ["reduce", 6 * f + 1, f"reduce{6 * f}", 2.0, 0.2],
            ["reduce", 6 * f + 2, f"reduce{6 * f + 1}", 0.0, 0.3],
            ["reduce", 6 * f + 3, f"reduce{6 * f + 2}", 0.0, 0.3],
            ["reduce", 6 * f + 4, f"reduce{6 * f + 3}", 3.0, 0.3],
            ["reduce", 6 * f + 5, f"reduce{6 * f + 4}", 4.0, 0.3],
        ]
    tasks.append(["held", 0, "scale1", 0.0, 2.0])
    sources = [p for p in arrivals if p not in [(f, 0, 0) for f in range(N_CHUNK)]]
    waiting = [(f, 0, 0) for f in range(N_CHUNK)] + sources
    count = dict.fromkeys(range(N_CHUNK), 0)
    done, steps, now = {}, [], 0.0
    while left or tasks or waiting:
        for lane in lanes:
            busy[lane] = [e for e in busy[lane] if e > now]
        pick = None
        for k in left:
            lane = units[k][:2]
            if len(busy[lane]) < 5 and all(arrived.get(p, 1e9) <= now for p in units[k][4]):
                pick = k
                break
        if pick is not None:
            lane = units[pick][:2]
            free[lane] = max(free[lane], now) + length[pick]
            busy[lane].append(free[lane])
            arrived[pick] = free[lane] + hop
            left.remove(pick)
            steps.append(("send", pick))
            now += 0.08
            continue
        task = next((t for t in tasks if t[2] is None and t[3] <= now or t[2] in done and done[t[2]] + t[3] <= now), None)
        if task is not None:
            tasks.remove(task)
            steps.append((task[0], task[1]))
            now += task[4]
            done[f"{task[0]}{task[1]}"] = now
            continue
        picked = None
        if "scale1" in done:
            for f in range(N_CHUNK):
                ready = [p for p in waiting if p[0] == f and all(arrived.get(k, 1e9) <= now for k in arrivals[p])]
                remaining = sum(p[0] == f for p in waiting)
                if len(ready) >= GROUP or ready and len(ready) == remaining:
                    ready.sort(key=lambda p: max([arrived[k] for k in arrivals[p]], default=0.0))
                    picked = ready[:GROUP]
                    break
        if picked:
            for p in picked:
                waiting.remove(p)
            f = picked[0][0]
            steps.append(("multiply", (f, tuple(p[1:] for p in picked), count[f] == 0)))
            count[f] += len(picked)
            now += cost
            if not any(p[0] == f for p in waiting):
                done[f"all{f}"] = now
            continue
        now += 0.05
    return units, arrivals, steps, now


def kernel(
    plan, inv, cols_s, count_s, feats_h, memory_h, tiles_h, cols_h, conv_w, conv_b, in_w, in_b, hid_w, hid_b, out,
    panel, tiles, acc, sums, deg_out, deg_in, scales, cw, iw, hw, held, own,
    s1, r1, s2, r2, s3, r3, message, memory_v, cols_v, cb, ib, hb,
    send_sem, recv_sem, dsem_s, dsem_r, load_sem, rs_s, rs_r,
):
    units, arrivals, steps = plan
    index = {k: i for i, k in enumerate(units)}
    slots, tile = tiles_h.shape[2], tiles_h.shape[3]
    block_rows, width = feats_h.shape
    wide = width // N_CHUNK
    n_col, n_row = NX * NZ, 2 * NY
    col_blocks = n_col * block_rows // tile
    group_rows = n_row * block_rows
    row_blocks = group_rows // tile
    r = lax.axis_index("row")
    c = lax.axis_index("col")
    x, z = lax.div(c, NZ), lax.rem(c, NZ)
    y, core = lax.div(r, 2), lax.rem(r, 2)

    def col_at(dx, dz):
        return lax.rem(x + (dx + NX), NX) * NZ + lax.rem(z + (dz + NZ), NZ)

    def row_at(dy, other):
        return lax.rem(y + (dy + NY), NY) * 2 + (1 - core if other else core)

    half_slots = slots // 2
    moves = {f"own{f}": (feats_h.at[:, pl.ds(f * wide, wide)], panel.at[f, c]) for f in range(N_CHUNK)}
    moves["cols"] = (cols_h, cols_v)
    for i in range(2):
        part = pl.ds(i * half_slots, half_slots)
        moves[f"tiles{i}"] = (tiles_h.at[0, 0, part], tiles.at[part])
    moves |= {"memory": (memory_h, memory_v), "hid_w": (hid_w, hw), "hid_b": (hid_b, hb)}
    moves |= {"conv_w": (conv_w, cw), "conv_b": (conv_b, cb), "in_w": (in_w, iw), "in_b": (in_b, ib)}
    loads = {k: pltpu.make_async_copy(*ends, load_sem.at[i]) for i, (k, ends) in enumerate(moves.items())}
    for copy in loads.values():
        copy.start()

    barrier = pltpu.get_barrier_semaphore()

    @pl.loop(1, n_col)
    def _(i):
        pl.semaphore_signal(barrier, inc=1, device_id=(r, lax.rem(c + i, n_col)), device_id_type=MESH)

    for dy, other in ((0, True), (1, False), (-1, False)):
        pl.semaphore_signal(barrier, inc=1, device_id=(row_at(dy, other), c), device_id_type=MESH)
    for f in range(N_CHUNK):
        loads[f"own{f}"].wait()
    pl.semaphore_wait(barrier, n_col - 1 + 3)

    def arrival(key):
        f, _, dx, dz, _ = key
        _, _, lo, hi, _ = units[key]
        spot = panel.at[f, col_at(dx, dz), pl.ds(lo, hi - lo)]
        i = index[key]
        return pltpu.make_async_remote_copy(
            spot, spot, send_sem.at[i], recv_sem.at[i], device_id=(r, c), device_id_type=MESH
        )

    def sending(key):
        f, _, dx, dz, _ = key
        axis, sign, lo, hi, _ = units[key]
        sx, sz = (sign, 0) if axis == "x" else (0, sign)
        spot = panel.at[f, col_at(dx - sx, dz - sz), pl.ds(lo, hi - lo)]
        i = index[key]
        return pltpu.make_async_remote_copy(
            spot, spot, send_sem.at[i], recv_sem.at[i], device_id=(r, col_at(-sx, -sz)), device_id_type=MESH
        )

    waited = set()

    def wait_for(keys):
        for k in keys:
            if k not in waited:
                waited.add(k)
                arrival(k).wait_recv()

    def column_sums(part):
        loads[f"tiles{part}"].wait()

        @pl.loop(0, half_slots // 8)
        def _(g):
            t0 = pl.multiple_of(part * half_slots + g * 8, 8)
            rows = [jnp.sum(tiles[t0 + k].astype(F32), axis=0, keepdims=True) for k in range(8)]
            sums[pl.ds(t0, 8), :] = jnp.concatenate(rows, axis=0)

    def degree_send(i, first):
        peer = lax.rem(c + i, n_col)
        if first:
            src, dst = deg_out.at[pl.ds(2 * peer, 2)], deg_in.at[c]
        else:
            src = dst = scales.at[pl.ds(2 * c, 2)]
        k = 0 if first else 1
        return pltpu.make_async_remote_copy(
            src, dst, dsem_s.at[k, i], dsem_r.at[k, i], device_id=(r, peer), device_id_type=MESH
        )

    def degrees(part):
        if part == 0:
            loads["cols"].wait()
            block = lax.broadcasted_iota(jnp.int32, (col_blocks, slots), 0)
            slot = lax.broadcasted_iota(jnp.int32, (col_blocks, slots), 1)
            picker = jnp.where((cols_v[0] == block) & (slot < count_s[0, 0]), 1.0, 0.0).astype(F32)
            terms = jnp.dot(picker, sums[...], precision=lax.Precision.HIGHEST, preferred_element_type=F32)
            for b in range(col_blocks):
                deg_out[b] = terms[b : b + 1, :]
            deg_in[c] = deg_out[pl.ds(2 * c, 2)]

            @pl.loop(1, n_col)
            def _(i):
                degree_send(i, True).start()
        else:

            @pl.loop(1, n_col)
            def _(i):
                degree_send(i, True).wait_recv()

            total = jnp.sum(deg_in[...], axis=0)
            scales[pl.ds(2 * c, 2)] = lax.rsqrt(1.0 + total)

            @pl.loop(1, n_col)
            def _(i):
                degree_send(i, False).start()

    def scale(part):
        if part == 0:

            @pl.loop(1, n_col)
            def _(i):
                degree_send(i, False).wait_recv()

            tiles[slots] = jnp.zeros((tile, tile), BF16)

        @pl.loop(0, half_slots // 4)
        def _(g):
            for k in range(4):
                t = part * half_slots + g * 4 + k
                tiles[t] = (tiles[t].astype(F32) * scales[cols_s[0, 0, t]]).astype(BF16)

    def multiply(f, places, first):
        m_blocks = row_blocks // 2
        spots = [col_at(*place) for place in places]

        @pl.loop(0, row_blocks // m_blocks)
        def _(m):
            lhs = []
            for a in range(m_blocks):
                blocks = [tiles[inv[(m * m_blocks + a) * col_blocks + (2 * s + k)]] for s in spots for k in range(2)]
                lhs.append(jnp.concatenate(blocks, axis=1))
            rhs = jnp.concatenate([panel[f, s] for s in spots], axis=0)
            term = jnp.dot(jnp.concatenate(lhs, axis=0), rhs, preferred_element_type=F32)
            rows = pl.ds(pl.multiple_of(m * (m_blocks * tile), m_blocks * tile), m_blocks * tile)
            if first:
                acc[f, rows] = term
            else:
                acc[f, rows] += term

    half = block_rows // 2

    def owner_rows(rr, part=None):
        start = pl.multiple_of(rr * block_rows, block_rows)
        if part is None:
            return pl.ds(start, block_rows)
        return pl.ds(start + part * half, half)

    order = (2, 1, -1, 0)

    def rs_core(f, k):
        return pltpu.make_async_remote_copy(
            s1.at[f, k], r1.at[f, k], rs_s.at[f, k], rs_r.at[f, k], device_id=(row_at(0, True), c), device_id_type=MESH
        )

    def rs_first(f, up, k):
        i = 4 + 2 * up + k
        return pltpu.make_async_remote_copy(
            s2.at[f, up, k], r2.at[f, up, k], rs_s.at[f, i], rs_r.at[f, i],
            device_id=(row_at(1 - 2 * up, False), c), device_id_type=MESH,
        )

    def rs_second(f, up):
        return pltpu.make_async_remote_copy(
            s3.at[f, up], r3.at[f, up], rs_s.at[f, 8 + up], rs_r.at[f, 8 + up],
            device_id=(row_at(1 - 2 * up, False), c), device_id_type=MESH,
        )

    def pair(f, dy, part):
        k = order.index(dy)
        return acc[f, owner_rows(row_at(dy, False), part)] + r1[f, k, part * half : (part + 1) * half].astype(F32)

    def reduce(f, stage):
        if stage == 0:
            for k, dy in enumerate(order):
                s1[f, k] = acc[f, owner_rows(row_at(dy, True))].astype(BF16)
                rs_core(f, k).start()
        elif stage == 1:
            rs_core(f, 0).wait_recv()
            for up in (0, 1):
                s2[f, up, 0] = pair(f, 2, up).astype(BF16)
                rs_first(f, up, 0).start()
        elif stage == 2:
            for up in (0, 1):
                rs_core(f, 1 + up).wait_recv()
                s2[f, up, 1] = pair(f, 1 - 2 * up, 1 - up).astype(BF16)
                rs_first(f, up, 1).start()
        elif stage == 3:
            rs_core(f, 3).wait_recv()
            for up in (0, 1):
                own[f, up] = pair(f, 1 - 2 * up, up)
                own[f, 2 + up] = pair(f, 0, up)
        elif stage == 4:
            for up in (0, 1):
                rs_first(f, up, 0).wait_recv()
                s3[f, up] = (own[f, up] + r2[f, up, 0].astype(F32)).astype(BF16)
                rs_second(f, up).start()
        else:
            for up in (0, 1):
                rs_first(f, up, 1).wait_recv()
                own[f, 3 - up] += r2[f, up, 1].astype(F32)
            for up in (0, 1):
                rs_second(f, up).wait_recv()
                own[f, 2 + up] += r3[f, up].astype(F32)

    def held_product():
        for name in ("memory", "hid_w", "hid_b"):
            loads[name].wait()
        bias = hb[...].reshape(1, -1)
        low = memory_v[...].astype(BF16)
        for j in range(3 * width // 256):
            part = slice(j * 256, (j + 1) * 256)
            term = jnp.dot(low, hw[:, part], preferred_element_type=F32) + bias[:, part]
            held[:, part] = term

    run = {
        "sums": column_sums,
        "degrees": degrees,
        "scale": scale,
        "held": lambda _: held_product(),
        "reduce": lambda k: reduce(k // 6, k % 6),
    }
    for what, arg in steps:
        if what == "send":
            wait_for(units[arg][4])
            sending(arg).start()
        elif what == "multiply":
            f, places, first = arg
            for place in places:
                wait_for(arrivals[(f, *place)])
            multiply(f, places, first)
        else:
            run[what](arg)

    for name in ("conv_w", "conv_b", "in_w", "in_b"):
        loads[name].wait()
    for part in (0, 1):
        rows = slice(part * half, (part + 1) * half)
        owned = [own[f, 2 + part] for f in range(N_CHUNK)]
        square = sum(jnp.sum(o * o, axis=1, keepdims=True) for o in owned) * (1.0 / width)
        root = jnp.sqrt(square + norm_epsilon)
        normed = jnp.concatenate([(o / root).astype(BF16) for o in owned], axis=1)
        value = jnp.dot(normed, cw[...], preferred_element_type=F32) + cb[...].reshape(1, -1)
        message[rows] = jnp.maximum(value, 0.0).astype(BF16)
    bias = ib[...].reshape(1, -1)
    told = message[...]
    for j in range(width // 256):
        low, mid, high = (slice(k * width + j * 256, k * width + (j + 1) * 256) for k in range(3))
        gates = [jnp.dot(told, iw[:, p], preferred_element_type=F32) + bias[:, p] for p in (low, mid, high)]
        reset = jax.nn.sigmoid(gates[0] + held[:, low])
        update = jax.nn.sigmoid(gates[1] + held[:, mid])
        candidate = jnp.tanh(gates[2] + reset * held[:, high])
        out[:, low] = (1.0 - update) * candidate + update * memory_v[:, low]

    for k in units:
        sending(k).wait_send()

    @pl.loop(1, n_col)
    def _(i):
        degree_send(i, True).wait_send()
        degree_send(i, False).wait_send()

    for f in range(N_CHUNK):
        for k in range(NY):
            rs_core(f, k).wait_send()
        for up in (0, 1):
            rs_first(f, up, 0).wait_send()
            rs_first(f, up, 1).wait_send()
            rs_second(f, up).wait_send()


def on_device(
    features, memory, tile_values, tile_rows, tile_cols, tile_count,
    conv_weight, conv_bias, input_weight, input_bias, hidden_weight, hidden_bias,
):
    own_rows, width = features.shape
    slots, tile = tile_values.shape[2], tile_values.shape[3]
    n_col, n_row = lax.axis_size("col"), lax.axis_size("row")
    row_blocks, col_blocks = own_rows * n_row // tile, own_rows * n_col // tile
    slot = jnp.arange(slots)
    key = jnp.where(slot < tile_count[0, 0], tile_rows[0, 0] * col_blocks + tile_cols[0, 0], -1)
    hit = key[None, :] == jnp.arange(row_blocks * col_blocks)[:, None]
    inv = slots + jnp.sum(jnp.where(hit, slot[None, :] - slots, 0), axis=1)
    units, arrivals, steps, _ = make_plan(own_rows, width)
    wide = width // N_CHUNK
    half = own_rows // 2
    n = len(units)
    smem = pl.BlockSpec(memory_space=pltpu.SMEM)
    vmem = pl.BlockSpec(memory_space=pltpu.VMEM)
    hbm = pl.BlockSpec(memory_space=pltpu.HBM)
    return pl.pallas_call(
        functools.partial(kernel, (units, arrivals, steps)),
        out_shape=jax.ShapeDtypeStruct((own_rows, width), F32),
        in_specs=[smem] * 3 + [hbm] * 10,
        out_specs=vmem,
        scratch_shapes=[
            pltpu.VMEM((N_CHUNK, n_col, own_rows, wide), BF16),
            pltpu.VMEM((slots + 1, tile, tile), BF16),
            pltpu.VMEM((N_CHUNK, n_row * own_rows, wide), F32),
            pltpu.VMEM((slots, tile), F32),
            pltpu.VMEM((col_blocks, 1, tile), F32),
            pltpu.VMEM((n_col, 2, 1, tile), F32),
            pltpu.VMEM((col_blocks, 1, tile), F32),
            pltpu.VMEM((width, width), BF16),
            pltpu.VMEM((width, 3 * width), BF16),
            pltpu.VMEM((width, 3 * width), BF16),
            pltpu.VMEM((own_rows, 3 * width), F32),
            pltpu.VMEM((N_CHUNK, 4, half, wide), F32),
            pltpu.VMEM((N_CHUNK, NY, own_rows, wide), BF16),
            pltpu.VMEM((N_CHUNK, NY, own_rows, wide), BF16),
            pltpu.VMEM((N_CHUNK, 2, 2, half, wide), BF16),
            pltpu.VMEM((N_CHUNK, 2, 2, half, wide), BF16),
            pltpu.VMEM((N_CHUNK, 2, half, wide), BF16),
            pltpu.VMEM((N_CHUNK, 2, half, wide), BF16),
            pltpu.VMEM((own_rows, width), BF16),
            pltpu.VMEM((own_rows, width), F32),
            pltpu.VMEM((1, 1, slots), jnp.int32),
            pltpu.VMEM((width,), F32),
            pltpu.VMEM((3 * width,), F32),
            pltpu.VMEM((3 * width,), F32),
            pltpu.SemaphoreType.DMA((n,)),
            pltpu.SemaphoreType.DMA((n,)),
            pltpu.SemaphoreType.DMA((2, n_col)),
            pltpu.SemaphoreType.DMA((2, n_col)),
            pltpu.SemaphoreType.DMA((20,)),
            pltpu.SemaphoreType.DMA((N_CHUNK, 10)),
            pltpu.SemaphoreType.DMA((N_CHUNK, 10)),
        ],
        compiler_params=pltpu.CompilerParams(
            collective_id=0, has_side_effects=True, vmem_limit_bytes=48 << 20
        ),
    )(
        inv, tile_cols, tile_count,
        *[
            pltpu.with_memory_space_constraint(a, pltpu.HBM)
            for a in (
                features, memory, tile_values, tile_cols,
                conv_weight, conv_bias, input_weight, input_bias, hidden_weight, hidden_bias,
            )
        ],
    )


def solution(mesh):
    placed = (
        P(("row", "col"), None),
        P(("col", "row"), None),
        P("row", "col", None, None, None),
        P("row", "col", None),
        P("row", "col", None),
        P("row", "col"),
        P(),
        P(),
        P(),
        P(),
        P(),
        P(),
    )
    return jax.shard_map(
        on_device, mesh=mesh, in_specs=placed, out_specs=P(("col", "row"), None), check_vma=False
    )
```

```python
import functools

import jax
import jax.numpy as jnp
from jax import lax
from jax.experimental import pallas as pl
from jax.experimental.pallas import tpu as pltpu
from jax.sharding import PartitionSpec as P

norm_epsilon = 1e-06
NX, NZ = 4, 8
NY = 4
ROWS_A = (96, 96)
N_CHUNK = 2
GROUP = 4
MESH = pl.DeviceIdType.MESH
F32 = jnp.float32
BF16 = jnp.bfloat16


def block_units(f, part, rows):
    lo, hi = rows
    mid = (lo + hi) // 2
    units, at = {}, {(0, 0): []}
    n1, n2 = (NX, NZ) if part == 0 else (NZ, NX)
    first, second = ("x", "z") if part == 0 else ("z", "x")

    def offset(d1, d2):
        return (d1, d2) if part == 0 else (d2, d1)

    def ring(axis, n, place):
        for d in range(1, n // 2):
            for sign in (1, -1):
                key = (f, part, *place(sign * d), 2)
                units[key] = (axis, sign, lo, hi, list(at[place(sign * (d - 1))]))
                at[place(sign * d)] = [key]
        far = place(n // 2)
        at[far] = []
        for half, (sign, a, b) in enumerate(((1, lo, mid), (-1, mid, hi))):
            key = (f, part, *far, half)
            units[key] = (axis, sign, a, b, list(at[place(sign * (n // 2 - 1))]))
            at[far].append(key)

    ring(first, n1, lambda d: offset(d, 0))
    for d1 in [0] + [s * d for d in range(1, n1 // 2) for s in (1, -1)] + [n1 // 2]:
        ring(second, n2, lambda d, d1=d1: offset(d1, d))
    return units, at


def make_plan(block_rows, width):
    units, arrivals = {}, {}
    for f in range(N_CHUNK):
        for part, rows in ((0, (0, ROWS_A[f])), (1, (ROWS_A[f], block_rows))):
            more, at = block_units(f, part, rows)
            units.update(more)
            for place, keys in at.items():
                arrivals.setdefault((f, *place), []).extend(keys)
    per_row = width // N_CHUNK * 2 * 2 / 90e3
    hop = 0.6
    length = {k: (u[3] - u[2]) * per_row for k, u in units.items()}
    after = {k: [] for k in units}
    for k, u in units.items():
        for p in u[4]:
            after[p].append(k)
    tail = {}

    def tail_of(k):
        if k not in tail:
            tail[k] = length[k] + hop + max([tail_of(j) for j in after[k]], default=0.0)
        return tail[k]

    order = sorted(units, key=lambda k: (k[0], -tail_of(k), k))
    lanes = [(a, s) for a in "xz" for s in (1, -1)]
    arrived, free, busy = {}, dict.fromkeys(lanes, 0.0), {lane: [] for lane in lanes}
    left = list(order)
    cost = 22.0 / (N_CHUNK * 32) * GROUP
    tasks = [
        ["sums", 0, None, 2.0, 1.0],
        ["sums", 1, "sums0", 0.0, 1.0],
        ["degrees", 0, "sums1", 0.0, 1.5],
        ["degrees", 1, "degrees0", 5.0, 1.5],
        ["scale", 0, "degrees1", 4.0, 1.0],
        ["scale", 1, "scale0", 0.0, 1.0],
    ]
    for f in range(N_CHUNK):
        tasks += [
            ["reduce", 6 * f, f"all{f}", 0.0, 0.5],
            ["reduce", 6 * f + 1, f"reduce{6 * f}", 2.0, 0.2],
            ["reduce", 6 * f + 2, f"reduce{6 * f + 1}", 0.0, 0.3],
            ["reduce", 6 * f + 3, f"reduce{6 * f + 2}", 0.0, 0.3],
            ["reduce", 6 * f + 4, f"reduce{6 * f + 3}", 3.0, 0.3],
            ["reduce", 6 * f + 5, f"reduce{6 * f + 4}", 4.0, 0.3],
        ]
    tasks.append(["held", 0, "scale1", 0.0, 2.0])
    sources = [p for p in arrivals if p not in [(f, 0, 0) for f in range(N_CHUNK)]]
    waiting = [(f, 0, 0) for f in range(N_CHUNK)] + sources
    count = dict.fromkeys(range(N_CHUNK), 0)
    done, steps, now = {}, [], 0.0
    while left or tasks or waiting:
        for lane in lanes:
            busy[lane] = [e for e in busy[lane] if e > now]
        pick = None
        for k in left:
            lane = units[k][:2]
            if len(busy[lane]) < 5 and all(arrived.get(p, 1e9) <= now for p in units[k][4]):
                pick = k
                break
        if pick is not None:
            lane = units[pick][:2]
            free[lane] = max(free[lane], now) + length[pick]
            busy[lane].append(free[lane])
            arrived[pick] = free[lane] + hop
            left.remove(pick)
            steps.append(("send", pick))
            now += 0.08
            continue
        task = next((t for t in tasks if t[2] is None and t[3] <= now or t[2] in done and done[t[2]] + t[3] <= now), None)
        if task is not None:
            tasks.remove(task)
            steps.append((task[0], task[1]))
            now += task[4]
            done[f"{task[0]}{task[1]}"] = now
            continue
        picked = None
        if "scale1" in done:
            for f in range(N_CHUNK):
                ready = [p for p in waiting if p[0] == f and all(arrived.get(k, 1e9) <= now for k in arrivals[p])]
                remaining = sum(p[0] == f for p in waiting)
                if len(ready) >= GROUP or ready and len(ready) == remaining:
                    ready.sort(key=lambda p: max([arrived[k] for k in arrivals[p]], default=0.0))
                    picked = ready[:GROUP]
                    break
        if picked:
            for p in picked:
                waiting.remove(p)
            f = picked[0][0]
            steps.append(("multiply", (f, tuple(p[1:] for p in picked), count[f] == 0)))
            count[f] += len(picked)
            now += cost
            if not any(p[0] == f for p in waiting):
                done[f"all{f}"] = now
            continue
        now += 0.05
    return units, arrivals, steps, now


def kernel(
    plan, inv, cols_s, count_s, feats_h, memory_h, tiles_h, cols_h, conv_w, conv_b, in_w, in_b, hid_w, hid_b, out,
    panel, tiles, acc, sums, deg_out, deg_in, scales, cw, iw, hw, held, own,
    s1, r1, s2, r2, s3, r3, message, memory_v, cols_v, cb, ib, hb,
    send_sem, recv_sem, dsem_s, dsem_r, load_sem, rs_s, rs_r,
):
    units, arrivals, steps = plan
    index = {k: i for i, k in enumerate(units)}
    slots, tile = tiles_h.shape[2], tiles_h.shape[3]
    block_rows, width = feats_h.shape
    wide = width // N_CHUNK
    n_col, n_row = NX * NZ, 2 * NY
    col_blocks = n_col * block_rows // tile
    group_rows = n_row * block_rows
    row_blocks = group_rows // tile
    r = lax.axis_index("row")
    c = lax.axis_index("col")
    x, z = lax.div(c, NZ), lax.rem(c, NZ)
    y, core = lax.div(r, 2), lax.rem(r, 2)

    def col_at(dx, dz):
        return lax.rem(x + (dx + NX), NX) * NZ + lax.rem(z + (dz + NZ), NZ)

    def row_at(dy, other):
        return lax.rem(y + (dy + NY), NY) * 2 + (1 - core if other else core)

    half_slots = slots // 2
    moves = {f"own{f}": (feats_h.at[:, pl.ds(f * wide, wide)], panel.at[f, c]) for f in range(N_CHUNK)}
    moves["cols"] = (cols_h, cols_v)
    for i in range(2):
        part = pl.ds(i * half_slots, half_slots)
        moves[f"tiles{i}"] = (tiles_h.at[0, 0, part], tiles.at[part])
    moves |= {"memory": (memory_h, memory_v), "hid_w": (hid_w, hw), "hid_b": (hid_b, hb)}
    moves |= {"conv_w": (conv_w, cw), "conv_b": (conv_b, cb), "in_w": (in_w, iw), "in_b": (in_b, ib)}
    loads = {k: pltpu.make_async_copy(*ends, load_sem.at[i]) for i, (k, ends) in enumerate(moves.items())}
    for copy in loads.values():
        copy.start()

    barrier = pltpu.get_barrier_semaphore()

    @pl.loop(1, n_col)
    def _(i):
        pl.semaphore_signal(barrier, inc=1, device_id=(r, lax.rem(c + i, n_col)), device_id_type=MESH)

    for dy, other in ((0, True), (1, False), (-1, False)):
        pl.semaphore_signal(barrier, inc=1, device_id=(row_at(dy, other), c), device_id_type=MESH)
    for f in range(N_CHUNK):
        loads[f"own{f}"].wait()
    pl.semaphore_wait(barrier, n_col - 1 + 3)

    def arrival(key):
        f, _, dx, dz, _ = key
        _, _, lo, hi, _ = units[key]
        spot = panel.at[f, col_at(dx, dz), pl.ds(lo, hi - lo)]
        i = index[key]
        return pltpu.make_async_remote_copy(
            spot, spot, send_sem.at[i], recv_sem.at[i], device_id=(r, c), device_id_type=MESH
        )

    def sending(key):
        f, _, dx, dz, _ = key
        axis, sign, lo, hi, _ = units[key]
        sx, sz = (sign, 0) if axis == "x" else (0, sign)
        spot = panel.at[f, col_at(dx - sx, dz - sz), pl.ds(lo, hi - lo)]
        i = index[key]
        return pltpu.make_async_remote_copy(
            spot, spot, send_sem.at[i], recv_sem.at[i], device_id=(r, col_at(-sx, -sz)), device_id_type=MESH
        )

    waited = set()

    def wait_for(keys):
        for k in keys:
            if k not in waited:
                waited.add(k)
                arrival(k).wait_recv()

    def column_sums(part):
        loads[f"tiles{part}"].wait()

        @pl.loop(0, half_slots // 8)
        def _(g):
            t0 = pl.multiple_of(part * half_slots + g * 8, 8)
            rows = [jnp.sum(tiles[t0 + k].astype(F32), axis=0, keepdims=True) for k in range(8)]
            sums[pl.ds(t0, 8), :] = jnp.concatenate(rows, axis=0)

    def degree_send(i, first):
        peer = lax.rem(c + i, n_col)
        if first:
            src, dst = deg_out.at[pl.ds(2 * peer, 2)], deg_in.at[c]
        else:
            src = dst = scales.at[pl.ds(2 * c, 2)]
        k = 0 if first else 1
        return pltpu.make_async_remote_copy(
            src, dst, dsem_s.at[k, i], dsem_r.at[k, i], device_id=(r, peer), device_id_type=MESH
        )

    def degrees(part):
        if part == 0:
            loads["cols"].wait()
            block = lax.broadcasted_iota(jnp.int32, (col_blocks, slots), 0)
            slot = lax.broadcasted_iota(jnp.int32, (col_blocks, slots), 1)
            picker = jnp.where((cols_v[0] == block) & (slot < count_s[0, 0]), 1.0, 0.0).astype(F32)
            terms = jnp.dot(picker, sums[...], precision=lax.Precision.HIGHEST, preferred_element_type=F32)
            for b in range(col_blocks):
                deg_out[b] = terms[b : b + 1, :]
            deg_in[c] = deg_out[pl.ds(2 * c, 2)]

            @pl.loop(1, n_col)
            def _(i):
                degree_send(i, True).start()
        else:

            @pl.loop(1, n_col)
            def _(i):
                degree_send(i, True).wait_recv()

            total = jnp.sum(deg_in[...], axis=0)
            scales[pl.ds(2 * c, 2)] = lax.rsqrt(1.0 + total)

            @pl.loop(1, n_col)
            def _(i):
                degree_send(i, False).start()

    def scale(part):
        if part == 0:

            @pl.loop(1, n_col)
            def _(i):
                degree_send(i, False).wait_recv()

            tiles[slots] = jnp.zeros((tile, tile), BF16)

        @pl.loop(0, half_slots // 4)
        def _(g):
            for k in range(4):
                t = part * half_slots + g * 4 + k
                tiles[t] = (tiles[t].astype(F32) * scales[cols_s[0, 0, t]]).astype(BF16)

    def multiply(f, places, first):
        m_blocks = row_blocks // 2
        spots = [col_at(*place) for place in places]

        @pl.loop(0, row_blocks // m_blocks)
        def _(m):
            lhs = []
            for a in range(m_blocks):
                blocks = [tiles[inv[(m * m_blocks + a) * col_blocks + (2 * s + k)]] for s in spots for k in range(2)]
                lhs.append(jnp.concatenate(blocks, axis=1))
            rhs = jnp.concatenate([panel[f, s] for s in spots], axis=0)
            term = jnp.dot(jnp.concatenate(lhs, axis=0), rhs, preferred_element_type=F32)
            rows = pl.ds(pl.multiple_of(m * (m_blocks * tile), m_blocks * tile), m_blocks * tile)
            if first:
                acc[f, rows] = term
            else:
                acc[f, rows] += term

    half = block_rows // 2

    def owner_rows(rr, part=None):
        start = pl.multiple_of(rr * block_rows, block_rows)
        if part is None:
            return pl.ds(start, block_rows)
        return pl.ds(start + part * half, half)

    order = (2, 1, -1, 0)

    def rs_core(f, k):
        return pltpu.make_async_remote_copy(
            s1.at[f, k], r1.at[f, k], rs_s.at[f, k], rs_r.at[f, k], device_id=(row_at(0, True), c), device_id_type=MESH
        )

    def rs_first(f, up, k):
        i = 4 + 2 * up + k
        return pltpu.make_async_remote_copy(
            s2.at[f, up, k], r2.at[f, up, k], rs_s.at[f, i], rs_r.at[f, i],
            device_id=(row_at(1 - 2 * up, False), c), device_id_type=MESH,
        )

    def rs_second(f, up):
        return pltpu.make_async_remote_copy(
            s3.at[f, up], r3.at[f, up], rs_s.at[f, 8 + up], rs_r.at[f, 8 + up],
            device_id=(row_at(1 - 2 * up, False), c), device_id_type=MESH,
        )

    def pair(f, dy, part):
        k = order.index(dy)
        return acc[f, owner_rows(row_at(dy, False), part)] + r1[f, k, part * half : (part + 1) * half].astype(F32)

    def reduce(f, stage):
        if stage == 0:
            for k, dy in enumerate(order):
                s1[f, k] = acc[f, owner_rows(row_at(dy, True))].astype(BF16)
                rs_core(f, k).start()
        elif stage == 1:
            rs_core(f, 0).wait_recv()
            for up in (0, 1):
                s2[f, up, 0] = pair(f, 2, up).astype(BF16)
                rs_first(f, up, 0).start()
        elif stage == 2:
            for up in (0, 1):
                rs_core(f, 1 + up).wait_recv()
                s2[f, up, 1] = pair(f, 1 - 2 * up, 1 - up).astype(BF16)
                rs_first(f, up, 1).start()
        elif stage == 3:
            rs_core(f, 3).wait_recv()
            for up in (0, 1):
                own[f, up] = pair(f, 1 - 2 * up, up)
                own[f, 2 + up] = pair(f, 0, up)
        elif stage == 4:
            for up in (0, 1):
                rs_first(f, up, 0).wait_recv()
                s3[f, up] = (own[f, up] + r2[f, up, 0].astype(F32)).astype(BF16)
                rs_second(f, up).start()
        else:
            for up in (0, 1):
                rs_first(f, up, 1).wait_recv()
                own[f, 3 - up] += r2[f, up, 1].astype(F32)
            for up in (0, 1):
                rs_second(f, up).wait_recv()
                own[f, 2 + up] += r3[f, up].astype(F32)

    def held_product():
        for name in ("memory", "hid_w", "hid_b"):
            loads[name].wait()
        bias = hb[...].reshape(1, -1)
        low = memory_v[...].astype(BF16)
        for j in range(3 * width // 256):
            part = slice(j * 256, (j + 1) * 256)
            term = jnp.dot(low, hw[:, part], preferred_element_type=F32) + bias[:, part]
            held[:, part] = term

    def sends_left():
        for k in units:
            sending(k).wait_send()

        @pl.loop(1, n_col)
        def _(i):
            degree_send(i, True).wait_send()
            degree_send(i, False).wait_send()

    run = {
        "sums": column_sums,
        "degrees": degrees,
        "scale": scale,
        "held": lambda _: held_product(),
        "reduce": lambda k: reduce(k // 6, k % 6),
    }
    for what, arg in steps:
        if what == "send":
            wait_for(units[arg][4])
            sending(arg).start()
        elif what == "multiply":
            f, places, first = arg
            for place in places:
                wait_for(arrivals[(f, *place)])
            multiply(f, places, first)
        else:
            if what == "reduce" and arg == 6 * N_CHUNK - 2:
                sends_left()
            run[what](arg)

    for name in ("conv_w", "conv_b", "in_w", "in_b"):
        loads[name].wait()
    for part in (0, 1):
        rows = slice(part * half, (part + 1) * half)
        owned = [own[f, 2 + part] for f in range(N_CHUNK)]
        square = sum(jnp.sum(o * o, axis=1, keepdims=True) for o in owned) * (1.0 / width)
        root = jnp.sqrt(square + norm_epsilon)
        normed = jnp.concatenate([(o / root).astype(BF16) for o in owned], axis=1)
        value = jnp.dot(normed, cw[...], preferred_element_type=F32) + cb[...].reshape(1, -1)
        message[rows] = jnp.maximum(value, 0.0).astype(BF16)
    bias = ib[...].reshape(1, -1)
    told = message[...]
    for j in range(width // 256):
        low, mid, high = (slice(k * width + j * 256, k * width + (j + 1) * 256) for k in range(3))
        gates = [jnp.dot(told, iw[:, p], preferred_element_type=F32) + bias[:, p] for p in (low, mid, high)]
        reset = jax.nn.sigmoid(gates[0] + held[:, low])
        update = jax.nn.sigmoid(gates[1] + held[:, mid])
        candidate = jnp.tanh(gates[2] + reset * held[:, high])
        out[:, low] = (1.0 - update) * candidate + update * memory_v[:, low]

    for f in range(N_CHUNK):
        for k in range(NY):
            rs_core(f, k).wait_send()
        for up in (0, 1):
            rs_first(f, up, 0).wait_send()
            rs_first(f, up, 1).wait_send()
            rs_second(f, up).wait_send()


def on_device(
    features, memory, tile_values, tile_rows, tile_cols, tile_count,
    conv_weight, conv_bias, input_weight, input_bias, hidden_weight, hidden_bias,
):
    own_rows, width = features.shape
    slots, tile = tile_values.shape[2], tile_values.shape[3]
    n_col, n_row = lax.axis_size("col"), lax.axis_size("row")
    row_blocks, col_blocks = own_rows * n_row // tile, own_rows * n_col // tile
    slot = jnp.arange(slots)
    key = jnp.where(slot < tile_count[0, 0], tile_rows[0, 0] * col_blocks + tile_cols[0, 0], -1)
    hit = key[None, :] == jnp.arange(row_blocks * col_blocks)[:, None]
    inv = slots + jnp.sum(jnp.where(hit, slot[None, :] - slots, 0), axis=1)
    units, arrivals, steps, _ = make_plan(own_rows, width)
    wide = width // N_CHUNK
    half = own_rows // 2
    n = len(units)
    smem = pl.BlockSpec(memory_space=pltpu.SMEM)
    vmem = pl.BlockSpec(memory_space=pltpu.VMEM)
    hbm = pl.BlockSpec(memory_space=pltpu.HBM)
    return pl.pallas_call(
        functools.partial(kernel, (units, arrivals, steps)),
        out_shape=jax.ShapeDtypeStruct((own_rows, width), F32),
        in_specs=[smem] * 3 + [hbm] * 10,
        out_specs=vmem,
        scratch_shapes=[
            pltpu.VMEM((N_CHUNK, n_col, own_rows, wide), BF16),
            pltpu.VMEM((slots + 1, tile, tile), BF16),
            pltpu.VMEM((N_CHUNK, n_row * own_rows, wide), F32),
            pltpu.VMEM((slots, tile), F32),
            pltpu.VMEM((col_blocks, 1, tile), F32),
            pltpu.VMEM((n_col, 2, 1, tile), F32),
            pltpu.VMEM((col_blocks, 1, tile), F32),
            pltpu.VMEM((width, width), BF16),
            pltpu.VMEM((width, 3 * width), BF16),
            pltpu.VMEM((width, 3 * width), BF16),
            pltpu.VMEM((own_rows, 3 * width), F32),
            pltpu.VMEM((N_CHUNK, 4, half, wide), F32),
            pltpu.VMEM((N_CHUNK, NY, own_rows, wide), BF16),
            pltpu.VMEM((N_CHUNK, NY, own_rows, wide), BF16),
            pltpu.VMEM((N_CHUNK, 2, 2, half, wide), BF16),
            pltpu.VMEM((N_CHUNK, 2, 2, half, wide), BF16),
            pltpu.VMEM((N_CHUNK, 2, half, wide), BF16),
            pltpu.VMEM((N_CHUNK, 2, half, wide), BF16),
            pltpu.VMEM((own_rows, width), BF16),
            pltpu.VMEM((own_rows, width), F32),
            pltpu.VMEM((1, 1, slots), jnp.int32),
            pltpu.VMEM((width,), F32),
            pltpu.VMEM((3 * width,), F32),
            pltpu.VMEM((3 * width,), F32),
            pltpu.SemaphoreType.DMA((n,)),
            pltpu.SemaphoreType.DMA((n,)),
            pltpu.SemaphoreType.DMA((2, n_col)),
            pltpu.SemaphoreType.DMA((2, n_col)),
            pltpu.SemaphoreType.DMA((20,)),
            pltpu.SemaphoreType.DMA((N_CHUNK, 10)),
            pltpu.SemaphoreType.DMA((N_CHUNK, 10)),
        ],
        compiler_params=pltpu.CompilerParams(
            collective_id=0, has_side_effects=True, vmem_limit_bytes=48 << 20
        ),
    )(
        inv, tile_cols, tile_count,
        *[
            pltpu.with_memory_space_constraint(a, pltpu.HBM)
            for a in (
                features, memory, tile_values, tile_cols,
                conv_weight, conv_bias, input_weight, input_bias, hidden_weight, hidden_bias,
            )
        ],
    )


def solution(mesh):
    placed = (
        P(("row", "col"), None),
        P(("col", "row"), None),
        P("row", "col", None, None, None),
        P("row", "col", None),
        P("row", "col", None),
        P("row", "col"),
        P(),
        P(),
        P(),
        P(),
        P(),
        P(),
    )
    return jax.shard_map(
        on_device, mesh=mesh, in_specs=placed, out_specs=P(("col", "row"), None), check_vma=False
    )
```
